32 devices in a mesh: gz: 8 (over z, y), gy: 4 (over x, core).
Axes of the slice: x: 2, y: 2, z: 4, core: 2. Of those that a mesh axis runs over, the one named last changes fastest.
Arguments:
- block: float32 [8, 64, 128, 256], P(None, 'gz', 'gy'), may hold values from -6 to 6
- conduct: float32 [64, 128, 256], P('gz', 'gy'), may hold values from 0.5 to 2
Outputs:
- basis: float32 [8, 64, 128, 256], P(None, 'gz', 'gy')
The draws below stay inside these ranges and needn't reach their ends.
All inputs are finite; a program needn't handle non-finite values.
Results may differ from the reference program's by a relative error of at most 0.00021.
Values sent between devices are 32-bit elements; how exact they have to be, the bound alone decides.
A program may use at most 128 MiB of HBM per device.

```python
import math
import jax
import jax.numpy as jnp
from jax import lax

VEC = 8
DEG = 4
NX = 256
NY = 128
NZ = 64


def steps_of(rng, shape, pieces, low, high):
    gain, own = 1.0, jax.random.fold_in(rng, 6)
    for position, shards_of in pieces:
        steps = jnp.exp(jax.random.uniform(jax.random.fold_in(own, position), (shards_of,), jnp.float32, low / len(pieces), high / len(pieces)))
        gain = gain * jnp.repeat(steps, shape[position] // shards_of).reshape([-1 if axis == position else 1 for axis in range(len(shape))])
    return gain


def gaussian(stream_key, extent, width, reach, split=(), held_as=jnp.bfloat16):
    result = jax.random.normal(stream_key, extent, jnp.float32) * width
    if len(split) > 0:
        result = steps_of(stream_key, extent, split, -0.22, 0.18) * result
    return jnp.clip(result, min=-reach, max=reach).astype(held_as)


def setup_inputs(seed: int = 0) -> dict:
    key_of = jax.random.split(jax.random.key(seed), 3)
    return {
        "block": gaussian(key_of[0], (VEC, NZ, NY, NX), 1.0, 6.0, ((1, 8), (2, 4)), jnp.float32),
        "conduct": jnp.clip(jnp.exp(math.log(2.0) - 1.3862944 * jax.random.uniform(key_of[1], (NZ, NY, NX), jnp.float32) ** steps_of(key_of[1], (NZ, NY, NX), ((0, 8), (1, 4)), -0.2, 0.2)), 0.5, 2.0),
    }


mid_point = 12.75
half_width = 11.25

def stencil(padded, kpadded):
    inner = slice(1, -1)
    centre = padded[:, 1:-1, 1:-1, 1:-1]
    kcentre = kpadded[1:-1, 1:-1, 1:-1]
    shifts = [(slice(2, None), inner, inner), (slice(None, -2), inner, inner), (inner, slice(2, None), inner), (inner, slice(None, -2), inner), (inner, inner, slice(2, None)), (inner, inner, slice(None, -2))]
    total = jnp.zeros_like(centre)
    for where in shifts:
        total = total + 0.5 * (kcentre + kpadded[where]) * (centre - padded[(slice(None),) + where])
    return total

def operate(field, conduct):
    padded = jnp.pad(field, ((0, 0), (1, 1), (1, 1), (1, 1)))
    kpadded = jnp.pad(conduct, 1)
    return stencil(padded, kpadded)

def reference(block, conduct):
    field = block
    for passes in range(2):
        previous = field
        current = (operate(field, conduct) - mid_point * field) / half_width
        for step in range(DEG - 1):
            nextone = 2.0 * (operate(current, conduct) - mid_point * current) / half_width - previous
            previous = current
            current = nextone
        field = current
    vectors = field.shape[0]
    flat = field.reshape(vectors, -1)
    gram = jnp.dot(flat, flat.T, precision=lax.Precision.HIGHEST)
    lower = jnp.linalg.cholesky(gram)
    inverse = lax.linalg.triangular_solve(lower, jnp.eye(vectors, dtype=jnp.float32), left_side=True, lower=True)
    scaled = jnp.dot(inverse, flat, precision=lax.Precision.HIGHEST) * math.sqrt(flat.shape[1])
    return scaled.reshape(field.shape)
```

```python
import functools
import math

import jax
import jax.numpy as jnp
from jax import lax
from jax.experimental import pallas as pl
from jax.experimental.pallas import tpu as pltpu
from jax.sharding import PartitionSpec as P

DEG = 4
PASSES = 2
STEPS = DEG * PASSES
STRIDE = 2

mid_point = 12.75
half_width = 11.25


def kernel(
    nz, ny,
    block, conduct, filtered, gram_out,
    field, coef, wz, wym, wyp, wxm, wxp, diag,
    yhalo, ysend, gathered, pairs, gsum_y, gsum_z,
    zs, zr, ys, yr, xs, xr, xl, rs, rr, rl, gys, gyr, gzs, gzr, outs,
):
    g = lax.axis_index("gz")
    h = lax.axis_index("gy")
    part = lax.rem(g, 2)
    other = 1 - part
    partner = g + 1 - 2 * part
    vectors, planes, rows, columns = block.shape
    mine = vectors // 2
    deep = 2 * planes
    low_z, high_z = g >= 2, g < nz - 2
    low_y, high_y = h >= 1, h < ny - 1

    def remote(src, dst, send, recv, gz, gy):
        return pltpu.make_async_remote_copy(
            src_ref=src, dst_ref=dst, send_sem=send, recv_sem=recv,
            device_id={"gz": gz, "gy": gy}, device_id_type=pl.DeviceIdType.MESH,
        )

    barrier = pltpu.get_barrier_semaphore()
    for d in range(1, nz):
        pl.semaphore_signal(barrier, inc=1, device_id={"gz": lax.rem(g + d, nz), "gy": h}, device_id_type=pl.DeviceIdType.MESH)
    for d in range(1, ny):
        pl.semaphore_signal(barrier, inc=1, device_id={"gz": g, "gy": lax.rem(h + d, ny)}, device_id_type=pl.DeviceIdType.MESH)

    zero_plane = jnp.zeros((rows, columns), jnp.float32)
    zero_rows = jnp.zeros((deep, columns), jnp.float32)

    @pl.when(jnp.logical_not(low_z))
    def _():
        coef[0] = zero_plane
        for v in range(mine):
            for slot in range(2):
                field[v, slot, 0] = zero_plane

    @pl.when(jnp.logical_not(high_z))
    def _():
        coef[deep + 1] = zero_plane
        for v in range(mine):
            for slot in range(2):
                field[v, slot, deep + 1] = zero_plane

    @pl.when(jnp.logical_not(low_y))
    def _():
        for v in range(mine + 1):
            for slot in range(2):
                yhalo[v, slot, 0] = zero_rows

    @pl.when(jnp.logical_not(high_y))
    def _():
        for v in range(mine + 1):
            for slot in range(2):
                yhalo[v, slot, 1] = zero_rows

    here = pl.ds(1 + planes * part, planes)
    there = pl.ds(1 + planes * other, planes)
    local_c = pltpu.make_async_copy(conduct, coef.at[here], xl.at[mine])
    local_v = [
        pltpu.make_async_copy(block.at[mine * part + v], field.at[v, 0, here], xl.at[v])
        for v in range(mine)
    ]
    swap_c = remote(conduct, coef.at[here], xs.at[mine], xr.at[mine], partner, h)
    swap_v = [
        remote(block.at[mine * other + v], field.at[v, 0, here], xs.at[v], xr.at[v], partner, h)
        for v in range(mine)
    ]
    local_c.start()
    for v in range(mine):
        local_v[v].start()
    pl.semaphore_wait(barrier, nz + ny - 2)
    swap_c.start()
    for v in range(mine):
        swap_v[v].start()

    def edges(body, v, slot):
        return [
            (low_z, remote(body.at[1], body.at[deep + 1], zs.at[v, slot, 0], zr.at[v, slot, 1], g - 2, h)),
            (high_z, remote(body.at[deep], body.at[0], zs.at[v, slot, 1], zr.at[v, slot, 0], g + 2, h)),
            (low_y, remote(ysend.at[v, slot, 0], yhalo.at[v, slot, 1], ys.at[v, slot, 0], yr.at[v, slot, 1], g, h - 1)),
            (high_y, remote(ysend.at[v, slot, 1], yhalo.at[v, slot, 0], ys.at[v, slot, 1], yr.at[v, slot, 0], g, h + 1)),
        ]

    def arrivals(body, v, slot):
        return [
            (high_z, remote(body.at[1], body.at[deep + 1], zs.at[v, slot, 0], zr.at[v, slot, 1], g + 2, h)),
            (low_z, remote(body.at[deep], body.at[0], zs.at[v, slot, 1], zr.at[v, slot, 0], g - 2, h)),
            (high_y, remote(ysend.at[v, slot, 0], yhalo.at[v, slot, 1], ys.at[v, slot, 0], yr.at[v, slot, 1], g, h + 1)),
            (low_y, remote(ysend.at[v, slot, 1], yhalo.at[v, slot, 0], ys.at[v, slot, 1], yr.at[v, slot, 0], g, h - 1)),
        ]

    def send_edges(body, v, slot):
        for cond, copy in edges(body, v, slot):
            pl.when(cond)(copy.start)

    def sent_edges(body, v, slot):
        for cond, copy in edges(body, v, slot):
            pl.when(cond)(copy.wait_send)

    def got_edges(body, v, slot):
        for cond, copy in arrivals(body, v, slot):
            pl.when(cond)(copy.wait_recv)

    def take_rows(body, v, slot):
        @pl.loop(0, deep)
        def _(z):
            ysend[v, slot, 0, pl.ds(z, 1), :] = body[z + 1, 0:1, :]
            ysend[v, slot, 1, pl.ds(z, 1), :] = body[z + 1, rows - 1 : rows, :]

    row_id = lax.broadcasted_iota(jnp.int32, (rows, columns), 0)
    col_id = lax.broadcasted_iota(jnp.int32, (rows, columns), 1)

    def y_neighbours(plane, v, slot, z):
        below = jnp.where(row_id == 0, yhalo[v, slot, 0, pl.ds(z, 1), :], pltpu.roll(plane, 1, 0))
        above = jnp.where(row_id == rows - 1, yhalo[v, slot, 1, pl.ds(z, 1), :], pltpu.roll(plane, rows - 1, 0))
        return below, above

    def x_neighbours(plane):
        return pltpu.roll(plane, 1, 1), pltpu.roll(plane, columns - 1, 1)

    local_c.wait()
    swap_c.wait_recv()
    take_rows(coef, mine, 0)
    send_edges(coef, mine, 0)
    got_edges(coef, mine, 0)
    scale = 1.0 / half_width
    wz[0] = scale * (coef[0] + coef[1])

    @pl.loop(0, deep)
    def _(z):
        plane = coef[z + 1]
        below, above = y_neighbours(plane, mine, 0, z)
        left, right = x_neighbours(plane)
        left = jnp.where(col_id == 0, 0.0, left)
        right = jnp.where(col_id == columns - 1, 0.0, right)
        zp = scale * (plane + coef[z + 2])
        zm = scale * (plane + coef[z])
        yp = scale * (plane + above)
        ym = scale * (plane + below)
        xp = scale * (plane + right)
        xm = scale * (plane + left)
        wz[z + 1] = zp
        wyp[z] = yp
        wym[z] = ym
        wxp[z] = jnp.where(col_id == columns - 1, 0.0, xp)
        wxm[z] = jnp.where(col_id == 0, 0.0, xm)
        diag[z] = (zp + zm) + (yp + ym) + (xp + xm) - (2.0 * mid_point / half_width)

    def advance(v, step):
        slot, later = step % 2, (step + 1) % 2
        now, nxt = field.at[v, slot], field.at[v, later]
        first = step % DEG == 0
        if step >= 1:
            sent_edges(nxt, v, later)
        got_edges(now, v, slot)

        @pl.loop(0, deep)
        def _(z):
            plane = now[z + 1]
            below, above = y_neighbours(plane, v, slot, z)
            left, right = x_neighbours(plane)
            total = diag[z] * plane
            total -= wz[z] * now[z] + wz[z + 1] * now[z + 2]
            total -= wym[z] * below + wyp[z] * above
            total -= wxm[z] * left + wxp[z] * right
            if first:
                total = 0.5 * total
            else:
                total = total - nxt[z + 1]
            nxt[z + 1] = total
            if step < STEPS - 1:
                ysend[v, later, 0, pl.ds(z, 1), :] = total[0:1, :]
                ysend[v, later, 1, pl.ds(z, 1), :] = total[rows - 1 : rows, :]

        if step < STEPS - 1:
            send_edges(nxt, v, later)

    def give_back(v):
        return remote(field.at[v, STEPS % 2, there], gathered.at[mine * part + v], rs.at[v], rr.at[v], partner, h)

    def keep(v):
        return pltpu.make_async_copy(field.at[v, STEPS % 2, here], gathered.at[mine * part + v], rl.at[v])

    for tick in range(STEPS + 1 + STRIDE * (mine - 1)):
        for v in range(mine):
            step = tick - STRIDE * v - 1
            if step == -1:
                local_v[v].wait()
                swap_v[v].wait_recv()
                take_rows(field.at[v, 0], v, 0)
                send_edges(field.at[v, 0], v, 0)
            elif 0 <= step < STEPS:
                advance(v, step)
                if step == STEPS - 1:
                    give_back(v).start()
                    keep(v).start()

    for v in range(mine):
        keep(v).wait()
        remote(field.at[v, STEPS % 2, there], gathered.at[mine * other + v], rs.at[v], rr.at[v], partner, h).wait_recv()
    to_out = pltpu.make_async_copy(gathered, filtered, outs)
    to_out.start()

    index = [(i, j) for i in range(vectors) for j in range(i + 1)]
    tiles = rows // 8

    def gram_body(t, accs):
        z, r = t // tiles, pl.multiple_of((t % tiles) * 8, 8)
        accs = list(accs)
        for c in range(columns // 128):
            vals = [gathered[v, z, pl.ds(r, 8), c * 128 : (c + 1) * 128] for v in range(vectors)]
            for p, (i, j) in enumerate(index):
                accs[p] = accs[p] + vals[i] * vals[j]
        return tuple(accs)

    accs = lax.fori_loop(0, planes * tiles, gram_body, tuple(jnp.zeros((8, 128), jnp.float32) for _ in index))
    pairs[...] = jnp.zeros((128, 128), jnp.float32)
    for p, (i, j) in enumerate(index):
        line = jnp.sum(accs[p], axis=0, keepdims=True)
        pairs[i * vectors + j : i * vectors + j + 1, :] = line
        if i != j:
            pairs[j * vectors + i : j * vectors + i + 1, :] = line
    ones = jnp.ones((8, 128), jnp.float32)
    part_sum = lax.dot_general(
        ones, pairs[...], (((1,), (1,)), ((), ())), precision=lax.Precision.HIGHEST,
        preferred_element_type=jnp.float32,
    )

    def total_of(value, slots, send, recv, axis, me, count):
        slots[me] = value
        copies = []
        for d in range(1, count):
            target = lax.rem(me + d, count)
            gz, gy = (target, h) if axis == "gz" else (g, target)
            copy = remote(slots.at[me], slots.at[me], send.at[d - 1], recv.at[d - 1], gz, gy)
            copy.start()
            copies.append(copy)
        for d in range(1, count):
            source = lax.rem(me - d + count, count)
            gz, gy = (source, h) if axis == "gz" else (g, source)
            remote(slots.at[source], slots.at[source], send.at[d - 1], recv.at[d - 1], gz, gy).wait_recv()
        result = slots[0]
        for d in range(1, count):
            result = result + slots[d]
        for copy in copies:
            copy.wait_send()
        return result

    slab = total_of(part_sum, gsum_y, gys, gyr, "gy", h, ny)
    gram_out[...] = total_of(slab, gsum_z, gzs, gzr, "gz", g, nz)

    swap_c.wait_send()
    sent_edges(coef, mine, 0)
    for v in range(mine):
        swap_v[v].wait_send()
        sent_edges(field.at[v, (STEPS - 1) % 2], v, (STEPS - 1) % 2)
        give_back(v).wait_send()
    to_out.wait()


def filter_and_gram(block, conduct):
    nz, ny = lax.axis_size("gz"), lax.axis_size("gy")
    vectors, planes, rows, columns = block.shape
    mine, deep = vectors // 2, 2 * planes
    f32 = jnp.float32
    dma = pltpu.SemaphoreType.DMA
    volume = pltpu.VMEM((deep, rows, columns), f32)
    return pl.pallas_call(
        functools.partial(kernel, nz, ny),
        out_shape=[jax.ShapeDtypeStruct(block.shape, f32), jax.ShapeDtypeStruct((8, 128), f32)],
        in_specs=[pl.BlockSpec(memory_space=pl.ANY)] * 2,
        out_specs=[pl.BlockSpec(memory_space=pl.ANY), pl.BlockSpec(memory_space=pltpu.VMEM)],
        scratch_shapes=[
            pltpu.VMEM((mine, 2, deep + 2, rows, columns), f32),
            pltpu.VMEM((deep + 2, rows, columns), f32),
            pltpu.VMEM((deep + 1, rows, columns), f32),
            volume, volume, volume, volume, volume,
            pltpu.VMEM((mine + 1, 2, 2, deep, columns), f32),
            pltpu.VMEM((mine + 1, 2, 2, deep, columns), f32),
            pltpu.VMEM((vectors, planes, rows, columns), f32),
            pltpu.VMEM((128, 128), f32),
            pltpu.VMEM((ny, 8, 128), f32),
            pltpu.VMEM((nz, 8, 128), f32),
            dma((mine + 1, 2, 2)), dma((mine + 1, 2, 2)), dma((mine + 1, 2, 2)), dma((mine + 1, 2, 2)),
            dma((mine + 1,)), dma((mine + 1,)), dma((mine + 1,)),
            dma((mine,)), dma((mine,)), dma((mine,)),
            dma((ny,)), dma((ny,)), dma((nz,)), dma((nz,)),
            dma,
        ],
        compiler_params=pltpu.CompilerParams(
            collective_id=0, has_side_effects=True, vmem_limit_bytes=40 * 1024 * 1024
        ),
        name="filter_and_gram",
    )(block, conduct)


def shards(block, conduct):
    vectors, planes, rows, columns = block.shape
    field, sums = filter_and_gram(block, conduct)
    gram = sums[0, : vectors * vectors].reshape(vectors, vectors)
    lower = jnp.linalg.cholesky(gram)
    inverse = lax.linalg.triangular_solve(
        lower, jnp.eye(vectors, dtype=jnp.float32), left_side=True, lower=True
    )
    total_cells = columns * rows * planes * lax.axis_size("gz") * lax.axis_size("gy")
    flat = field.reshape(vectors, -1)
    scaled = jnp.dot(inverse * math.sqrt(total_cells), flat, precision=lax.Precision.HIGHEST)
    return scaled.reshape(field.shape)


def solution(mesh):
    in_specs = (P(None, "gz", "gy", None), P("gz", "gy", None))
    out_specs = P(None, "gz", "gy", None)
    return jax.shard_map(shards, mesh=mesh, in_specs=in_specs, out_specs=out_specs, check_vma=False)
```

```python
import functools
import math

import jax
import jax.numpy as jnp
from jax import lax
from jax.experimental import pallas as pl
from jax.experimental.pallas import tpu as pltpu
from jax.sharding import PartitionSpec as P

DEG = 4
PASSES = 2
STEPS = DEG * PASSES
UNROLL = 7
MODEL = (14.0, 5.7, 2.3, 0.5)

mid_point = 12.75
half_width = 11.25


def task_order(count):
    first, apart, trip, work = MODEL
    ready = [first + apart * v for v in range(count)]
    step = [-1] * count
    now, order = 0.0, []
    while min(step) < STEPS:
        v = min((u for u in range(count) if step[u] < STEPS), key=lambda u: (max(ready[u], now), ready[u], u))
        now = max(now, ready[v]) + (work if step[v] >= 0 else 0.1)
        ready[v] = now + trip
        order.append((v, step[v]))
        step[v] += 1
    return order


def kernel(
    nz, ny,
    block, conduct, filtered, gram_out,
    field, coef, wz, wym, wyp, wxm, wxp, diag,
    yhalo, ysend, gathered, pairs, gsum_y, gsum_z,
    zs, zr, ys, yr, xs, xr, xl, rs, rr, rl, gys, gyr, gzs, gzr, outs,
):
    g = lax.axis_index("gz")
    h = lax.axis_index("gy")
    part = lax.rem(g, 2)
    other = 1 - part
    partner = g + 1 - 2 * part
    vectors, planes, rows, columns = block.shape
    mine = vectors // 2
    deep = 2 * planes
    low_z, high_z = g >= 2, g < nz - 2
    low_y, high_y = h >= 1, h < ny - 1

    def remote(src, dst, send, recv, gz, gy):
        return pltpu.make_async_remote_copy(
            src_ref=src, dst_ref=dst, send_sem=send, recv_sem=recv,
            device_id={"gz": gz, "gy": gy}, device_id_type=pl.DeviceIdType.MESH,
        )

    barrier = pltpu.get_barrier_semaphore()
    for d in range(1, nz):
        pl.semaphore_signal(barrier, inc=1, device_id={"gz": lax.rem(g + d, nz), "gy": h}, device_id_type=pl.DeviceIdType.MESH)
    for d in range(1, ny):
        pl.semaphore_signal(barrier, inc=1, device_id={"gz": g, "gy": lax.rem(h + d, ny)}, device_id_type=pl.DeviceIdType.MESH)

    zero_plane = jnp.zeros((rows, columns), jnp.float32)
    zero_rows = jnp.zeros((deep, columns), jnp.float32)

    @pl.when(jnp.logical_not(low_z))
    def _():
        coef[0] = zero_plane
        for v in range(mine):
            for slot in range(2):
                field[v, slot, 0] = zero_plane

    @pl.when(jnp.logical_not(high_z))
    def _():
        coef[deep + 1] = zero_plane
        for v in range(mine):
            for slot in range(2):
                field[v, slot, deep + 1] = zero_plane

    @pl.when(jnp.logical_not(low_y))
    def _():
        for v in range(mine + 1):
            for slot in range(2):
                yhalo[v, slot, 0] = zero_rows

    @pl.when(jnp.logical_not(high_y))
    def _():
        for v in range(mine + 1):
            for slot in range(2):
                yhalo[v, slot, 1] = zero_rows

    here = pl.ds(1 + planes * part, planes)
    there = pl.ds(1 + planes * other, planes)
    local_c = pltpu.make_async_copy(conduct, coef.at[here], xl.at[mine])
    local_v = [
        pltpu.make_async_copy(block.at[mine * part + v], field.at[v, 0, here], xl.at[v])
        for v in range(mine)
    ]
    swap_c = remote(conduct, coef.at[here], xs.at[mine], xr.at[mine], partner, h)
    swap_v = [
        remote(block.at[mine * other + v], field.at[v, 0, here], xs.at[v], xr.at[v], partner, h)
        for v in range(mine)
    ]
    local_c.start()
    for v in range(mine):
        local_v[v].start()
    pl.semaphore_wait(barrier, nz + ny - 2)
    swap_c.start()
    for v in range(mine):
        swap_v[v].start()

    def edges(body, v, slot):
        return [
            (low_z, remote(body.at[1], body.at[deep + 1], zs.at[v, slot, 0], zr.at[v, slot, 1], g - 2, h)),
            (high_z, remote(body.at[deep], body.at[0], zs.at[v, slot, 1], zr.at[v, slot, 0], g + 2, h)),
            (low_y, remote(ysend.at[v, slot, 0], yhalo.at[v, slot, 1], ys.at[v, slot, 0], yr.at[v, slot, 1], g, h - 1)),
            (high_y, remote(ysend.at[v, slot, 1], yhalo.at[v, slot, 0], ys.at[v, slot, 1], yr.at[v, slot, 0], g, h + 1)),
        ]

    def arrivals(body, v, slot):
        return [
            (high_z, remote(body.at[1], body.at[deep + 1], zs.at[v, slot, 0], zr.at[v, slot, 1], g + 2, h)),
            (low_z, remote(body.at[deep], body.at[0], zs.at[v, slot, 1], zr.at[v, slot, 0], g - 2, h)),
            (high_y, remote(ysend.at[v, slot, 0], yhalo.at[v, slot, 1], ys.at[v, slot, 0], yr.at[v, slot, 1], g, h + 1)),
            (low_y, remote(ysend.at[v, slot, 1], yhalo.at[v, slot, 0], ys.at[v, slot, 1], yr.at[v, slot, 0], g, h - 1)),
        ]

    def send_z(body, v, slot):
        for cond, copy in edges(body, v, slot)[:2]:
            pl.when(cond)(copy.start)

    def send_y(body, v, slot):
        for cond, copy in edges(body, v, slot)[2:]:
            pl.when(cond)(copy.start)

    def sent_edges(body, v, slot):
        for cond, copy in edges(body, v, slot):
            pl.when(cond)(copy.wait_send)

    def got_edges(body, v, slot):
        for cond, copy in arrivals(body, v, slot):
            pl.when(cond)(copy.wait_recv)

    def take_rows(body, v, slot):
        @pl.loop(0, deep)
        def _(z):
            ysend[v, slot, 0, pl.ds(z, 1), :] = body[z + 1, 0:1, :]
            ysend[v, slot, 1, pl.ds(z, 1), :] = body[z + 1, rows - 1 : rows, :]

    row_id = lax.broadcasted_iota(jnp.int32, (rows, columns), 0)
    col_id = lax.broadcasted_iota(jnp.int32, (rows, columns), 1)

    def y_neighbours(plane, v, slot, z):
        below = jnp.where(row_id == 0, yhalo[v, slot, 0, pl.ds(z, 1), :], pltpu.roll(plane, 1, 0))
        above = jnp.where(row_id == rows - 1, yhalo[v, slot, 1, pl.ds(z, 1), :], pltpu.roll(plane, rows - 1, 0))
        return below, above

    def x_neighbours(plane):
        return pltpu.roll(plane, 1, 1), pltpu.roll(plane, columns - 1, 1)

    local_c.wait()
    swap_c.wait_recv()
    send_z(coef, mine, 0)
    take_rows(coef, mine, 0)
    send_y(coef, mine, 0)
    got_edges(coef, mine, 0)
    scale = 1.0 / half_width
    wz[0] = scale * (coef[0] + coef[1])

    @pl.loop(0, deep)
    def _(z):
        plane = coef[z + 1]
        below, above = y_neighbours(plane, mine, 0, z)
        left, right = x_neighbours(plane)
        left = jnp.where(col_id == 0, 0.0, left)
        right = jnp.where(col_id == columns - 1, 0.0, right)
        zp = scale * (plane + coef[z + 2])
        zm = scale * (plane + coef[z])
        yp = scale * (plane + above)
        ym = scale * (plane + below)
        xp = scale * (plane + right)
        xm = scale * (plane + left)
        wz[z + 1] = zp
        wyp[z] = yp
        wym[z] = ym
        wxp[z] = jnp.where(col_id == columns - 1, 0.0, xp)
        wxm[z] = jnp.where(col_id == 0, 0.0, xm)
        diag[z] = (zp + zm) + (yp + ym) + (xp + xm) - (2.0 * mid_point / half_width)

    def advance(v, step):
        slot, later = step % 2, (step + 1) % 2
        now, nxt = field.at[v, slot], field.at[v, later]
        first = step % DEG == 0
        if step >= 1:
            sent_edges(nxt, v, later)
        got_edges(now, v, slot)

        def one_plane(z):
            plane = now[z + 1]
            below, above = y_neighbours(plane, v, slot, z)
            left, right = x_neighbours(plane)
            total = diag[z] * plane
            total -= wz[z] * now[z] + wz[z + 1] * now[z + 2]
            total -= wym[z] * below + wyp[z] * above
            total -= wxm[z] * left + wxp[z] * right
            if first:
                total = 0.5 * total
            else:
                total = total - nxt[z + 1]
            nxt[z + 1] = total
            if step < STEPS - 1:
                ysend[v, later, 0, pl.ds(z, 1), :] = total[0:1, :]
                ysend[v, later, 1, pl.ds(z, 1), :] = total[rows - 1 : rows, :]

        one_plane(0)
        one_plane(deep - 1)
        if step < STEPS - 1:
            send_z(nxt, v, later)
        pl.loop(1, deep - 1, unroll=UNROLL)(one_plane)
        if step < STEPS - 1:
            send_y(nxt, v, later)

    def give_back(v):
        return remote(field.at[v, STEPS % 2, there], gathered.at[mine * part + v], rs.at[v], rr.at[v], partner, h)

    def keep(v):
        return pltpu.make_async_copy(field.at[v, STEPS % 2, here], gathered.at[mine * part + v], rl.at[v])

    for v, step in task_order(mine):
        if step < 0:
            local_v[v].wait()
            swap_v[v].wait_recv()
            send_z(field.at[v, 0], v, 0)
            take_rows(field.at[v, 0], v, 0)
            send_y(field.at[v, 0], v, 0)
        else:
            advance(v, step)
            if step == STEPS - 1:
                give_back(v).start()
                keep(v).start()

    for v in range(mine):
        keep(v).wait()
        remote(field.at[v, STEPS % 2, there], gathered.at[mine * other + v], rs.at[v], rr.at[v], partner, h).wait_recv()
    to_out = pltpu.make_async_copy(gathered, filtered, outs)
    to_out.start()

    index = [(i, j) for i in range(vectors) for j in range(i + 1)]
    tiles = rows // 8

    def gram_body(t, accs):
        z, r = t // tiles, pl.multiple_of((t % tiles) * 8, 8)
        accs = list(accs)
        for c in range(columns // 128):
            vals = [gathered[v, z, pl.ds(r, 8), c * 128 : (c + 1) * 128] for v in range(vectors)]
            for p, (i, j) in enumerate(index):
                accs[p] = accs[p] + vals[i] * vals[j]
        return tuple(accs)

    accs = lax.fori_loop(0, planes * tiles, gram_body, tuple(jnp.zeros((8, 128), jnp.float32) for _ in index))
    pairs[...] = jnp.zeros((128, 128), jnp.float32)
    for p, (i, j) in enumerate(index):
        line = jnp.sum(accs[p], axis=0, keepdims=True)
        pairs[i * vectors + j : i * vectors + j + 1, :] = line
        if i != j:
            pairs[j * vectors + i : j * vectors + i + 1, :] = line
    ones = jnp.ones((8, 128), jnp.float32)
    part_sum = lax.dot_general(
        ones, pairs[...], (((1,), (1,)), ((), ())), precision=lax.Precision.HIGHEST,
        preferred_element_type=jnp.float32,
    )

    def total_of(value, slots, send, recv, axis, me, count):
        slots[me] = value
        copies = []
        for d in range(1, count):
            target = lax.rem(me + d, count)
            gz, gy = (target, h) if axis == "gz" else (g, target)
            copy = remote(slots.at[me], slots.at[me], send.at[d - 1], recv.at[d - 1], gz, gy)
            copy.start()
            copies.append(copy)
        for d in range(1, count):
            source = lax.rem(me - d + count, count)
            gz, gy = (source, h) if axis == "gz" else (g, source)
            remote(slots.at[source], slots.at[source], send.at[d - 1], recv.at[d - 1], gz, gy).wait_recv()
        result = slots[0]
        for d in range(1, count):
            result = result + slots[d]
        for copy in copies:
            copy.wait_send()
        return result

    slab = total_of(part_sum, gsum_y, gys, gyr, "gy", h, ny)
    gram_out[...] = total_of(slab, gsum_z, gzs, gzr, "gz", g, nz)

    swap_c.wait_send()
    sent_edges(coef, mine, 0)
    for v in range(mine):
        swap_v[v].wait_send()
        sent_edges(field.at[v, (STEPS - 1) % 2], v, (STEPS - 1) % 2)
        give_back(v).wait_send()
    to_out.wait()


def filter_and_gram(block, conduct):
    nz, ny = lax.axis_size("gz"), lax.axis_size("gy")
    vectors, planes, rows, columns = block.shape
    mine, deep = vectors // 2, 2 * planes
    f32 = jnp.float32
    dma = pltpu.SemaphoreType.DMA
    volume = pltpu.VMEM((deep, rows, columns), f32)
    return pl.pallas_call(
        functools.partial(kernel, nz, ny),
        out_shape=[jax.ShapeDtypeStruct(block.shape, f32), jax.ShapeDtypeStruct((8, 128), f32)],
        in_specs=[pl.BlockSpec(memory_space=pl.ANY)] * 2,
        out_specs=[pl.BlockSpec(memory_space=pl.ANY), pl.BlockSpec(memory_space=pltpu.VMEM)],
        scratch_shapes=[
            pltpu.VMEM((mine, 2, deep + 2, rows, columns), f32),
            pltpu.VMEM((deep + 2, rows, columns), f32),
            pltpu.VMEM((deep + 1, rows, columns), f32),
            volume, volume, volume, volume, volume,
            pltpu.VMEM((mine + 1, 2, 2, deep, columns), f32),
            pltpu.VMEM((mine + 1, 2, 2, deep, columns), f32),
            pltpu.VMEM((vectors, planes, rows, columns), f32),
            pltpu.VMEM((128, 128), f32),
            pltpu.VMEM((ny, 8, 128), f32),
            pltpu.VMEM((nz, 8, 128), f32),
            dma((mine + 1, 2, 2)), dma((mine + 1, 2, 2)), dma((mine + 1, 2, 2)), dma((mine + 1, 2, 2)),
            dma((mine + 1,)), dma((mine + 1,)), dma((mine + 1,)),
            dma((mine,)), dma((mine,)), dma((mine,)),
            dma((ny,)), dma((ny,)), dma((nz,)), dma((nz,)),
            dma,
        ],
        compiler_params=pltpu.CompilerParams(
            collective_id=0, has_side_effects=True, vmem_limit_bytes=60 * 1024 * 1024
        ),
        name="filter_and_gram",
    )(block, conduct)


def finish_kernel(cells, sums, field, basis, inverse):
    vectors = field.shape[0]

    @pl.when(pl.program_id(0) == 0)
    def _():
        gram = sums[...]
        low = {}
        recip = []
        for j in range(vectors):
            for i in range(j, vectors):
                at = i * vectors + j
                value = jnp.broadcast_to(gram[:, at : at + 1], (8, 128))
                for k in range(j):
                    value = value - low[i, k] * low[j, k]
                if i == j:
                    low[j, j] = jnp.sqrt(value)
                    recip.append(1.0 / low[j, j])
                else:
                    low[i, j] = value * recip[j]
        for j in range(vectors):
            column = {j: recip[j]}
            for i in range(j + 1, vectors):
                value = low[i, j] * column[j]
                for k in range(j + 1, i):
                    value = value + low[i, k] * column[k]
                column[i] = -value * recip[i]
            for i in range(j, vectors):
                inverse[i * vectors + j] = column[i] * math.sqrt(cells)

    factors = {(i, j): inverse[i * vectors + j] for i in range(vectors) for j in range(i + 1)}
    rows, columns = field.shape[2:]
    for r in range(0, rows, 8):
        for c in range(0, columns, 128):
            vals = [field[v, 0, r : r + 8, c : c + 128] for v in range(vectors)]
            for i in range(vectors):
                total = factors[i, 0] * vals[0]
                for j in range(1, i + 1):
                    total = total + factors[i, j] * vals[j]
                basis[i, 0, r : r + 8, c : c + 128] = total


def shards(block, conduct):
    vectors, planes, rows, columns = block.shape
    field, sums = filter_and_gram(block, conduct)
    total_cells = columns * rows * planes * lax.axis_size("gz") * lax.axis_size("gy")
    spec = pl.BlockSpec((vectors, 1, rows, columns), lambda z: (0, z, 0, 0))
    return pl.pallas_call(
        functools.partial(finish_kernel, total_cells),
        grid=(planes,),
        out_shape=jax.ShapeDtypeStruct(block.shape, jnp.float32),
        in_specs=[pl.BlockSpec((8, 128), lambda z: (0, 0)), spec],
        out_specs=spec,
        scratch_shapes=[pltpu.VMEM((vectors * vectors, 8, 128), jnp.float32)],
        name="finish",
    )(sums, field)


def solution(mesh):
    in_specs = (P(None, "gz", "gy", None), P("gz", "gy", None))
    out_specs = P(None, "gz", "gy", None)
    return jax.shard_map(shards, mesh=mesh, in_specs=in_specs, out_specs=out_specs, check_vma=False)
```

```python
import functools
import math

import jax
import jax.numpy as jnp
from jax import lax
from jax.experimental import pallas as pl
from jax.experimental.pallas import tpu as pltpu
from jax.sharding import PartitionSpec as P

DEG = 4
PASSES = 2
STEPS = DEG * PASSES
UNROLL = 7
MODEL = (14.0, 5.7, 2.8, 0.6)

mid_point = 12.75
half_width = 11.25


def task_order(count):
    first, apart, trip, work = MODEL
    ready = [first + apart * v for v in range(count)]
    step = [-1] * count
    now, order = 0.0, []
    while min(step) < STEPS:
        v = min((u for u in range(count) if step[u] < STEPS), key=lambda u: (max(ready[u], now), ready[u], u))
        now = max(now, ready[v]) + (work if step[v] >= 0 else 0.1)
        ready[v] = now + trip
        order.append((v, step[v]))
        step[v] += 1
    return order


def kernel(
    nz, ny,
    block, conduct, filtered, gram_out,
    field, coef, wz, wym, wyp, wxm, wxp, diag,
    yhalo, ysend, gathered, pairs, gsum_y, gsum_z,
    outbox, outbox_c,
    bl, zs, zr, ys, yr, xs, xr, xl, rs, rr, rl, gys, gyr, gzs, gzr, outs,
):
    g = lax.axis_index("gz")
    h = lax.axis_index("gy")
    part = lax.rem(g, 2)
    other = 1 - part
    partner = g + 1 - 2 * part
    vectors, planes, rows, columns = block.shape
    mine = vectors // 2
    deep = 2 * planes
    low_z, high_z = g >= 2, g < nz - 2
    low_y, high_y = h >= 1, h < ny - 1

    def remote(src, dst, send, recv, gz, gy):
        return pltpu.make_async_remote_copy(
            src_ref=src, dst_ref=dst, send_sem=send, recv_sem=recv,
            device_id={"gz": gz, "gy": gy}, device_id_type=pl.DeviceIdType.MESH,
        )

    barrier = pltpu.get_barrier_semaphore()
    for d in range(1, nz):
        pl.semaphore_signal(barrier, inc=1, device_id={"gz": lax.rem(g + d, nz), "gy": h}, device_id_type=pl.DeviceIdType.MESH)
    for d in range(1, ny):
        pl.semaphore_signal(barrier, inc=1, device_id={"gz": g, "gy": lax.rem(h + d, ny)}, device_id_type=pl.DeviceIdType.MESH)

    zero_plane = jnp.zeros((rows, columns), jnp.float32)
    zero_rows = jnp.zeros((deep, columns), jnp.float32)

    @pl.when(jnp.logical_not(low_z))
    def _():
        coef[0] = zero_plane
        for v in range(mine):
            for slot in range(2):
                field[v, slot, 0] = zero_plane

    @pl.when(jnp.logical_not(high_z))
    def _():
        coef[deep + 1] = zero_plane
        for v in range(mine):
            for slot in range(2):
                field[v, slot, deep + 1] = zero_plane

    @pl.when(jnp.logical_not(low_y))
    def _():
        for v in range(mine + 1):
            for slot in range(2):
                yhalo[v, slot, 0] = zero_rows

    @pl.when(jnp.logical_not(high_y))
    def _():
        for v in range(mine + 1):
            for slot in range(2):
                yhalo[v, slot, 1] = zero_rows

    here = pl.ds(1 + planes * part, planes)
    there = pl.ds(1 + planes * other, planes)
    local_c = pltpu.make_async_copy(conduct, coef.at[here], xl.at[mine])
    local_v = [
        pltpu.make_async_copy(block.at[mine * part + v], field.at[v, 0, here], xl.at[v])
        for v in range(mine)
    ]
    load_c = pltpu.make_async_copy(conduct, outbox_c, bl.at[mine])
    load_v = [
        pltpu.make_async_copy(block.at[mine * other + v], outbox.at[v], bl.at[v])
        for v in range(mine)
    ]
    swap_c = remote(outbox_c, coef.at[here], xs.at[mine], xr.at[mine], partner, h)
    swap_v = [
        remote(outbox.at[v], field.at[v, 0, here], xs.at[v], xr.at[v], partner, h)
        for v in range(mine)
    ]
    load_c.start()
    for v in range(mine):
        load_v[v].start()
    local_c.start()
    for v in range(mine):
        local_v[v].start()
    pl.semaphore_wait(barrier, nz + ny - 2)
    load_c.wait()
    swap_c.start()
    for v in range(mine):
        load_v[v].wait()
        swap_v[v].start()

    def edges(body, v, slot):
        return [
            (low_z, remote(body.at[1], body.at[deep + 1], zs.at[v, slot, 0], zr.at[v, slot, 1], g - 2, h)),
            (high_z, remote(body.at[deep], body.at[0], zs.at[v, slot, 1], zr.at[v, slot, 0], g + 2, h)),
            (low_y, remote(ysend.at[v, slot, 0], yhalo.at[v, slot, 1], ys.at[v, slot, 0], yr.at[v, slot, 1], g, h - 1)),
            (high_y, remote(ysend.at[v, slot, 1], yhalo.at[v, slot, 0], ys.at[v, slot, 1], yr.at[v, slot, 0], g, h + 1)),
        ]

    def arrivals(body, v, slot):
        return [
            (high_z, remote(body.at[1], body.at[deep + 1], zs.at[v, slot, 0], zr.at[v, slot, 1], g + 2, h)),
            (low_z, remote(body.at[deep], body.at[0], zs.at[v, slot, 1], zr.at[v, slot, 0], g - 2, h)),
            (high_y, remote(ysend.at[v, slot, 0], yhalo.at[v, slot, 1], ys.at[v, slot, 0], yr.at[v, slot, 1], g, h + 1)),
            (low_y, remote(ysend.at[v, slot, 1], yhalo.at[v, slot, 0], ys.at[v, slot, 1], yr.at[v, slot, 0], g, h - 1)),
        ]

    def send_z(body, v, slot):
        for cond, copy in edges(body, v, slot)[:2]:
            pl.when(cond)(copy.start)

    def send_y(body, v, slot):
        for cond, copy in edges(body, v, slot)[2:]:
            pl.when(cond)(copy.start)

    def sent_edges(body, v, slot):
        for cond, copy in edges(body, v, slot):
            pl.when(cond)(copy.wait_send)

    def got_edges(body, v, slot):
        for cond, copy in arrivals(body, v, slot):
            pl.when(cond)(copy.wait_recv)

    def take_rows(body, v, slot):
        @pl.loop(0, deep)
        def _(z):
            ysend[v, slot, 0, pl.ds(z, 1), :] = body[z + 1, 0:1, :]
            ysend[v, slot, 1, pl.ds(z, 1), :] = body[z + 1, rows - 1 : rows, :]

    row_id = lax.broadcasted_iota(jnp.int32, (rows, columns), 0)
    col_id = lax.broadcasted_iota(jnp.int32, (rows, columns), 1)

    def y_neighbours(plane, v, slot, z):
        below = jnp.where(row_id == 0, yhalo[v, slot, 0, pl.ds(z, 1), :], pltpu.roll(plane, 1, 0))
        above = jnp.where(row_id == rows - 1, yhalo[v, slot, 1, pl.ds(z, 1), :], pltpu.roll(plane, rows - 1, 0))
        return below, above

    def x_neighbours(plane):
        return pltpu.roll(plane, 1, 1), pltpu.roll(plane, columns - 1, 1)

    local_c.wait()
    swap_c.wait_recv()
    send_z(coef, mine, 0)
    take_rows(coef, mine, 0)
    send_y(coef, mine, 0)
    got_edges(coef, mine, 0)
    scale = 1.0 / half_width
    wz[0] = scale * (coef[0] + coef[1])

    @pl.loop(0, deep)
    def _(z):
        plane = coef[z + 1]
        below, above = y_neighbours(plane, mine, 0, z)
        left, right = x_neighbours(plane)
        left = jnp.where(col_id == 0, 0.0, left)
        right = jnp.where(col_id == columns - 1, 0.0, right)
        zp = scale * (plane + coef[z + 2])
        zm = scale * (plane + coef[z])
        yp = scale * (plane + above)
        ym = scale * (plane + below)
        xp = scale * (plane + right)
        xm = scale * (plane + left)
        wz[z + 1] = zp
        wyp[z] = yp
        wym[z] = ym
        wxp[z] = jnp.where(col_id == columns - 1, 0.0, xp)
        wxm[z] = jnp.where(col_id == 0, 0.0, xm)
        diag[z] = (zp + zm) + (yp + ym) + (xp + xm) - (2.0 * mid_point / half_width)

    def advance(v, step):
        slot, later = step % 2, (step + 1) % 2
        now, nxt = field.at[v, slot], field.at[v, later]
        first = step % DEG == 0
        if step >= 1:
            sent_edges(nxt, v, later)
        got_edges(now, v, slot)

        def one_plane(z):
            plane = now[z + 1]
            below, above = y_neighbours(plane, v, slot, z)
            left, right = x_neighbours(plane)
            total = diag[z] * plane
            total -= wz[z] * now[z] + wz[z + 1] * now[z + 2]
            total -= wym[z] * below + wyp[z] * above
            total -= wxm[z] * left + wxp[z] * right
            if first:
                total = 0.5 * total
            else:
                total = total - nxt[z + 1]
            nxt[z + 1] = total
            if step < STEPS - 1:
                ysend[v, later, 0, pl.ds(z, 1), :] = total[0:1, :]
                ysend[v, later, 1, pl.ds(z, 1), :] = total[rows - 1 : rows, :]

        one_plane(0)
        one_plane(deep - 1)
        if step < STEPS - 1:
            send_z(nxt, v, later)
        pl.loop(1, deep - 1, unroll=UNROLL)(one_plane)
        if step < STEPS - 1:
            send_y(nxt, v, later)

    def give_back(v):
        return remote(field.at[v, STEPS % 2, there], gathered.at[mine * part + v], rs.at[v], rr.at[v], partner, h)

    def keep(v):
        return pltpu.make_async_copy(field.at[v, STEPS % 2, here], gathered.at[mine * part + v], rl.at[v])

    for v, step in task_order(mine):
        if step < 0:
            local_v[v].wait()
            swap_v[v].wait_recv()
            send_z(field.at[v, 0], v, 0)
            take_rows(field.at[v, 0], v, 0)
            send_y(field.at[v, 0], v, 0)
        else:
            advance(v, step)
            if step == STEPS - 1:
                give_back(v).start()
                keep(v).start()

    for v in range(mine):
        keep(v).wait()
        remote(field.at[v, STEPS % 2, there], gathered.at[mine * other + v], rs.at[v], rr.at[v], partner, h).wait_recv()
    to_out = pltpu.make_async_copy(gathered, filtered, outs)
    to_out.start()

    index = [(i, j) for i in range(vectors) for j in range(i + 1)]
    tiles = rows // 8

    def gram_body(t, accs):
        z, r = t // tiles, pl.multiple_of((t % tiles) * 8, 8)
        accs = list(accs)
        for c in range(columns // 128):
            vals = [gathered[v, z, pl.ds(r, 8), c * 128 : (c + 1) * 128] for v in range(vectors)]
            for p, (i, j) in enumerate(index):
                accs[p] = accs[p] + vals[i] * vals[j]
        return tuple(accs)

    accs = lax.fori_loop(0, planes * tiles, gram_body, tuple(jnp.zeros((8, 128), jnp.float32) for _ in index))
    pairs[...] = jnp.zeros((128, 128), jnp.float32)
    for p, (i, j) in enumerate(index):
        line = jnp.sum(accs[p], axis=0, keepdims=True)
        pairs[i * vectors + j : i * vectors + j + 1, :] = line
        if i != j:
            pairs[j * vectors + i : j * vectors + i + 1, :] = line
    ones = jnp.ones((8, 128), jnp.float32)
    part_sum = lax.dot_general(
        ones, pairs[...], (((1,), (1,)), ((), ())), precision=lax.Precision.HIGHEST,
        preferred_element_type=jnp.float32,
    )

    def total_of(value, slots, send, recv, axis, me, count):
        slots[me] = value
        copies = []
        for d in range(1, count):
            target = lax.rem(me + d, count)
            gz, gy = (target, h) if axis == "gz" else (g, target)
            copy = remote(slots.at[me], slots.at[me], send.at[d - 1], recv.at[d - 1], gz, gy)
            copy.start()
            copies.append(copy)
        for d in range(1, count):
            source = lax.rem(me - d + count, count)
            gz, gy = (source, h) if axis == "gz" else (g, source)
            remote(slots.at[source], slots.at[source], send.at[d - 1], recv.at[d - 1], gz, gy).wait_recv()
        result = slots[0]
        for d in range(1, count):
            result = result + slots[d]
        for copy in copies:
            copy.wait_send()
        return result

    slab = total_of(part_sum, gsum_y, gys, gyr, "gy", h, ny)
    gram_out[...] = total_of(slab, gsum_z, gzs, gzr, "gz", g, nz)

    swap_c.wait_send()
    sent_edges(coef, mine, 0)
    for v in range(mine):
        swap_v[v].wait_send()
        sent_edges(field.at[v, (STEPS - 1) % 2], v, (STEPS - 1) % 2)
        give_back(v).wait_send()
    to_out.wait()


def filter_and_gram(block, conduct):
    nz, ny = lax.axis_size("gz"), lax.axis_size("gy")
    vectors, planes, rows, columns = block.shape
    mine, deep = vectors // 2, 2 * planes
    f32 = jnp.float32
    dma = pltpu.SemaphoreType.DMA
    volume = pltpu.VMEM((deep, rows, columns), f32)
    return pl.pallas_call(
        functools.partial(kernel, nz, ny),
        out_shape=[jax.ShapeDtypeStruct(block.shape, f32), jax.ShapeDtypeStruct((8, 128), f32)],
        in_specs=[pl.BlockSpec(memory_space=pl.ANY)] * 2,
        out_specs=[pl.BlockSpec(memory_space=pl.ANY), pl.BlockSpec(memory_space=pltpu.VMEM)],
        scratch_shapes=[
            pltpu.VMEM((mine, 2, deep + 2, rows, columns), f32),
            pltpu.VMEM((deep + 2, rows, columns), f32),
            pltpu.VMEM((deep + 1, rows, columns), f32),
            volume, volume, volume, volume, volume,
            pltpu.VMEM((mine + 1, 2, 2, deep, columns), f32),
            pltpu.VMEM((mine + 1, 2, 2, deep, columns), f32),
            pltpu.VMEM((vectors, planes, rows, columns), f32),
            pltpu.VMEM((128, 128), f32),
            pltpu.VMEM((ny, 8, 128), f32),
            pltpu.VMEM((nz, 8, 128), f32),
            pltpu.VMEM((mine, planes, rows, columns), f32),
            pltpu.VMEM((planes, rows, columns), f32),
            dma((mine + 1,)),
            dma((mine + 1, 2, 2)), dma((mine + 1, 2, 2)), dma((mine + 1, 2, 2)), dma((mine + 1, 2, 2)),
            dma((mine + 1,)), dma((mine + 1,)), dma((mine + 1,)),
            dma((mine,)), dma((mine,)), dma((mine,)),
            dma((ny,)), dma((ny,)), dma((nz,)), dma((nz,)),
            dma,
        ],
        compiler_params=pltpu.CompilerParams(
            collective_id=0, has_side_effects=True, vmem_limit_bytes=60 * 1024 * 1024
        ),
        name="filter_and_gram",
    )(block, conduct)


def finish_kernel(cells, sums, field, basis, held, result, taken, given):
    vectors, planes, rows, columns = field.shape
    take = [pltpu.make_async_copy(field.at[:, z], held.at[:, z], taken.at[z]) for z in range(planes)]
    give = [pltpu.make_async_copy(result.at[:, z], basis.at[:, z], given.at[z]) for z in range(planes)]
    for z in range(planes):
        take[z].start()
    gram = sums[...]
    low = {}
    factors = {}
    recip = []
    for j in range(vectors):
        for i in range(j, vectors):
            at = i * vectors + j
            value = jnp.broadcast_to(gram[:, at : at + 1], (8, 128))
            for k in range(j):
                value = value - low[i, k] * low[j, k]
            if i == j:
                low[j, j] = jnp.sqrt(value)
                recip.append(1.0 / low[j, j])
            else:
                low[i, j] = value * recip[j]
    for j in range(vectors):
        column = {j: recip[j]}
        for i in range(j + 1, vectors):
            value = low[i, j] * column[j]
            for k in range(j + 1, i):
                value = value + low[i, k] * column[k]
            column[i] = -value * recip[i]
        for i in range(j, vectors):
            factors[i, j] = column[i] * math.sqrt(cells)

    for z in range(planes):
        take[z].wait()

        @pl.loop(0, rows, step=8)
        def _(r):
            r = pl.multiple_of(r, 8)
            for c in range(0, columns, 128):
                vals = [held[v, z, pl.ds(r, 8), c : c + 128] for v in range(vectors)]
                for i in range(vectors):
                    total = factors[i, 0] * vals[0]
                    for j in range(1, i + 1):
                        total = total + factors[i, j] * vals[j]
                    result[i, z, pl.ds(r, 8), c : c + 128] = total

        give[z].start()
    for z in range(planes):
        give[z].wait()


def shards(block, conduct):
    vectors, planes, rows, columns = block.shape
    field, sums = filter_and_gram(block, conduct)
    total_cells = columns * rows * planes * lax.axis_size("gz") * lax.axis_size("gy")
    whole = pltpu.VMEM(block.shape, jnp.float32)
    return pl.pallas_call(
        functools.partial(finish_kernel, total_cells),
        out_shape=jax.ShapeDtypeStruct(block.shape, jnp.float32),
        in_specs=[pl.BlockSpec(memory_space=pltpu.VMEM), pl.BlockSpec(memory_space=pl.ANY)],
        out_specs=pl.BlockSpec(memory_space=pl.ANY),
        scratch_shapes=[whole, whole, pltpu.SemaphoreType.DMA((planes,)), pltpu.SemaphoreType.DMA((planes,))],
        compiler_params=pltpu.CompilerParams(vmem_limit_bytes=60 * 1024 * 1024),
        name="finish",
    )(sums, field)


def solution(mesh):
    in_specs = (P(None, "gz", "gy", None), P("gz", "gy", None))
    out_specs = P(None, "gz", "gy", None)
    return jax.shard_map(shards, mesh=mesh, in_specs=in_specs, out_specs=out_specs, check_vma=False)
```
